32 devices in a mesh: space: 4 (over y, core), vel: 8 (over z, x).
Axes of the slice: x: 2, y: 2, z: 4, core: 2. Of those that a mesh axis runs over, the one named last changes fastest.
Arguments:
- distribution: float32 [64, 48, 2304], P('space', 'vel'), may hold values from 0 to 2
- collision_rate: float32 [64], P('space'), may hold values from 0.1 to 1
- face_flags: int32 [64], replicated, may hold values 0 or 1
Outputs:
- updated: float32 [64, 48, 2304], P('space', 'vel')
The draws below stay inside these ranges and needn't reach their ends.
All inputs are finite; a program needn't handle non-finite values.
Results may differ from the reference program's by a relative error of at most 0.0001.
Values sent between devices are 32-bit elements; how exact they have to be, the bound alone decides.
A program may use at most 64 MiB of HBM per device.

```python
import math
import jax
import jax.numpy as jnp
from jax import lax

NV = 48
NCELLS = 64


def place_ends(array, own_key, smallest, high):
    longest = array.shape.index(max(array.shape))
    spots = []
    for shift in (0, 1):
        where = [jax.random.randint(jax.random.fold_in(own_key, axis), (), 0, length) for axis, length in enumerate(array.shape)]
        where[longest] = (where[longest] + shift) % array.shape[longest]
        spots.append(tuple(where))
    return array.at[spots[0]].set(smallest).at[spots[1]].set(high)


def steps_of(rng, extent, cuts, low, top_value):
    level, own = 1.0, jax.random.fold_in(rng, 6)
    for axis_at, parts in cuts:
        heights = jnp.exp(jax.random.uniform(jax.random.fold_in(own, axis_at), (parts,), jnp.float32, low / len(cuts), top_value / len(cuts)))
        level = level * jnp.repeat(heights, extent[axis_at] // parts).reshape([-1 if axis == axis_at else 1 for axis in range(len(extent))])
    return level


def setup_inputs(seed: int = 0) -> dict:
    key_list = jax.random.split(jax.random.key(seed), 4)
    distribution = jnp.clip(2.0 * jax.random.uniform(key_list[0], (NCELLS, NV, NV * NV), jnp.float32) ** steps_of(key_list[0], (NCELLS, NV, NV * NV), ((0, 4), (1, 8)), -0.2, 0.2), 0.0, 2.0)
    collision_rate = jnp.clip(jnp.exp(math.log(1.0) - 2.3025851 * jax.random.uniform(key_list[1], (NCELLS,), jnp.float32) ** steps_of(key_list[1], (NCELLS,), ((0, 4),), -0.2, 0.2)), 0.1, 1.0)
    face_flags = place_ends((jax.random.randint(key_list[2], (NCELLS,), 0, 16) < 1).astype(jnp.int32), jax.random.fold_in(key_list[2], 1), 0, 1)
    return dict(distribution=distribution, collision_rate=collision_rate, face_flags=face_flags)


LENGTH = 8.0
RADIUS = 6.0
COURANT = 0.9
GOLDEN = (1.0 + math.sqrt(5.0)) / 2.0
DIRECTIONS = ((0.0, 1.0, GOLDEN), (0.0, -1.0, GOLDEN), (1.0, GOLDEN, 0.0), (-1.0, GOLDEN, 0.0), (GOLDEN, 0.0, 1.0), (-GOLDEN, 0.0, 1.0))

def kernel_tables(points):
    index = jnp.arange(points, dtype=jnp.int32)
    wrapped = jnp.where(index < points // 2, index, jnp.where(index == points // 2, 0, index - points))
    signed = wrapped.astype(jnp.float32) * (math.pi / LENGTH)
    wave_z = signed[:, None, None]
    wave_x = signed[None, :, None]
    wave_y = signed[None, None, :]
    square = wave_x * wave_x + wave_y * wave_y + wave_z * wave_z
    scale = math.sqrt(1.0 + GOLDEN * GOLDEN)
    gain_tables = []
    loss_tables = []
    for direction in DIRECTIONS:
        parallel = (wave_x * direction[0] + wave_y * direction[1] + wave_z * direction[2]) / scale
        across = jnp.sqrt(jnp.maximum(square - parallel * parallel, 0.0))
        gain_tables.append(jnp.cos(0.5 * RADIUS * parallel))
        loss_tables.append(jnp.sinc(RADIUS * across / (2.0 * math.pi)))
    loss_total = sum(loss_tables) / 6.0
    return (gain_tables, loss_tables, loss_total)

def reference(distribution, collision_rate, face_flags):
    points = NV
    width = points * points
    cell_count = distribution.shape[0]
    gain_tables, loss_tables, loss_total = kernel_tables(points)

    def cell_term(one_cell):
        cube = one_cell.reshape(points, points, points)
        spectrum = jnp.fft.fftn(cube)
        products = []
        for gain_table, loss_table in zip(gain_tables, loss_tables):
            first_part = jnp.fft.ifftn(spectrum * gain_table).real
            second_part = jnp.fft.ifftn(spectrum * loss_table).real
            products.append(first_part * second_part)
        gain_total = sum(products) / 6.0
        loss_part = cube * jnp.fft.ifftn(spectrum * loss_total).real
        return (gain_total - loss_part).reshape(points, width)
    collision = lax.map(cell_term, distribution)
    mirror = distribution.reshape(cell_count, points, points, points)[:, :, ::-1, :].reshape(cell_count, points, width)
    previous = jnp.concatenate([distribution[:1], distribution[:-1]], axis=0)
    following = jnp.concatenate([distribution[1:], distribution[-1:]], axis=0)
    wall_flags = jnp.concatenate([face_flags, jnp.ones((1,), jnp.int32)])
    lower_wall = (wall_flags[:-1] == 1)[:, None, None]
    upper_wall = (wall_flags[1:] == 1)[:, None, None]
    lower_side = jnp.where(lower_wall, mirror, previous)
    upper_side = jnp.where(upper_wall, mirror, following)
    column = (jnp.arange(width, dtype=jnp.int32) // points).astype(jnp.float32)
    centre = (points - 1) / 2.0
    speed = COURANT * (column - centre) / centre
    upwind_flux = jnp.where(speed > 0, speed * (distribution - lower_side), speed * (upper_side - distribution))
    return distribution - upwind_flux + collision_rate[:, None, None] * collision
```

```python
import math

import jax
import jax.numpy as jnp
import ml_dtypes
import numpy as np
from jax import lax
from jax.experimental import pallas as pl
from jax.experimental.pallas import tpu as pltpu
from jax.sharding import PartitionSpec as P

NV = 48
LENGTH = 8.0
RADIUS = 6.0
COURANT = 0.9
GOLDEN = (1.0 + math.sqrt(5.0)) / 2.0
SCALE = math.sqrt(1.0 + GOLDEN * GOLDEN)
HALF = 64
LANES = 128
BF = jnp.bfloat16


def real_basis():
    j = np.arange(NV)
    q = np.zeros((NV, NV))
    for f in range(25):
        q[f] = np.cos(2 * np.pi * f * j / NV) * (1.0 if f in (0, 24) else math.sqrt(2.0))
    for f in range(1, 24):
        q[24 + f] = np.sin(2 * np.pi * f * j / NV) * math.sqrt(2.0)
    q /= math.sqrt(NV)
    odd = np.zeros((NV, NV))
    for f in range(1, 24):
        odd[:, f] = -q[24 + f]
        odd[:, 24 + f] = q[f]
    mag = np.concatenate([np.arange(24), [0], np.arange(1, 24)]) * (math.pi / LENGTH)
    return q, odd, mag


def circulants():
    j = np.arange(NV)
    k = np.where(j < 24, j, np.where(j == 24, 0, j - NV))
    xi = k * (math.pi / LENGTH)
    f = np.fft.fft(np.eye(NV), axis=0)

    def real(mult):
        return np.real(np.fft.ifft(mult[:, None] * f, axis=0))

    result = []
    for length in (1.0 / SCALE, GOLDEN / SCALE):
        angle = 0.5 * RADIUS * xi * length
        result.append((real(np.cos(angle)), real(1j * np.sin(angle))))
    return result


def split_np(w):
    w = np.asarray(w, np.float32)
    hi = w.astype(ml_dtypes.bfloat16)
    lo = (w - hi.astype(np.float32)).astype(ml_dtypes.bfloat16)
    return hi, lo


def left(w):
    hi, lo = split_np(w)
    return np.concatenate([hi, hi, lo], axis=1)


def right(w):
    full = np.zeros((LANES, LANES))
    full[:NV, :NV] = w.T
    full[HALF : HALF + NV, HALF : HALF + NV] = w.T
    hi, lo = split_np(full)
    return np.concatenate([hi, hi, lo], axis=0)


def build_tables():
    q, odd, mag = real_basis()
    (c1, d1), (c2, d2) = circulants()
    mz, mx, my = mag[:, None, None], mag[None, :, None], mag[None, None, :]
    square = mz * mz + mx * mx + my * my

    def sinc(p):
        return np.sinc(RADIUS * np.sqrt(np.maximum(square - p * p, 0.0)) / (2.0 * math.pi))

    plus, minus = [], []
    for first, second in ((my, mz), (mx, my), (mz, mx)):
        same = sinc((first + GOLDEN * second) / SCALE)
        other = sinc((GOLDEN * second - first) / SCALE)
        plus.append((same + other) / 6.0)
        minus.append((other - same) / 6.0)
    spec = np.zeros((6, NV, NV, LANES), np.float32)
    values = np.stack(plus + minus)
    spec[..., :NV] = values
    spec[..., HALF : HALF + NV] = values
    lefts = [q, q.T, odd, c1, d1, c2, d2]
    left_all = np.stack([left(w) for w in lefts])
    left_pair = left(np.concatenate([c2, d2], axis=0))
    right_first = np.concatenate([right(w) for w in (q, c2, d2)], axis=1)
    right_rest = np.stack([right(q.T), right(odd)])
    right_gain = np.concatenate([right(c1), right(d1)], axis=1)
    return spec, left_all, left_pair, right_first, right_rest, right_gain


def parts(x):
    hi = x.astype(BF)
    lo = (x - hi.astype(jnp.float32)).astype(BF)
    return hi, lo


def tall(x):
    hi, lo = parts(x)
    return jnp.concatenate([hi, lo, hi], axis=0)


def wide(x):
    hi, lo = parts(x)
    return jnp.concatenate([hi, lo, hi], axis=1)


def dot(a, b):
    return jnp.dot(a, b, preferred_element_type=jnp.float32)


def collide_kernel(
    u_in, spec_hbm, la, lp, rf, rr, rg, out, u, v, ey, fy, spec, fields, gains, sem
):
    cells = u_in.shape[0]
    load = pltpu.make_async_copy(spec_hbm, spec, sem)
    load.start()
    u[...] = jnp.zeros_like(u)
    for x in range(NV):
        for c in range(cells):
            u[x * NV : (x + 1) * NV, c * HALF : c * HALF + NV] = u_in[c, :, x * NV : (x + 1) * NV]

    def first(x, carry):
        rows = pl.ds(pl.multiple_of(x * NV, NV), NV)
        three = dot(wide(u[rows, :]), rf[...])
        ey[rows, :] = three[:, LANES : 2 * LANES]
        fy[rows, :] = three[:, 2 * LANES :]
        v[rows, :] = dot(la[0], tall(three[:, :LANES]))
        return carry

    lax.fori_loop(0, NV, first, 0, unroll=2)
    load.wait()

    def second(z, carry):
        rows = pl.ds(z, NV, stride=NV)
        s = dot(la[0], tall(v[rows, :]))
        hat = [tall(s * spec[f, z]) for f in range(6)]
        even = dot(la[1], jnp.concatenate(hat[:4], axis=1))
        odd = dot(la[2], jnp.concatenate(hat[4:], axis=1))
        for f in range(4):
            fields[f, rows, :] = even[:, f * LANES : (f + 1) * LANES]
        for f in range(2):
            fields[4 + f, rows, :] = odd[:, f * LANES : (f + 1) * LANES]
        pair = dot(lp[...], tall(u[rows, :]))
        gains[0, rows, :] = dot(la[3], tall(ey[rows, :]))
        gains[1, rows, :] = dot(la[4], tall(fy[rows, :]))
        gains[2, rows, :] = pair[:NV]
        gains[3, rows, :] = pair[NV:]
        return carry

    lax.fori_loop(0, NV, second, 0, unroll=2)

    def third(x, carry):
        rows = pl.ds(pl.multiple_of(x * NV, NV), NV)
        even_in = [wide(fields[f, rows, :]) for f in (0, 1, 2, 5)]
        odd_in = [wide(fields[f, rows, :]) for f in (3, 4)]
        even = dot(jnp.concatenate(even_in, axis=0), rr[0])
        odd = dot(jnp.concatenate(odd_in, axis=0), rr[1])
        plus = [even[f * NV : (f + 1) * NV] for f in range(3)]
        minus_zx = even[3 * NV :]
        minus_yz, minus_xy = odd[:NV], odd[NV:]
        straight = dot(
            la[1], jnp.concatenate([tall(p) for p in plus] + [tall(minus_xy)], axis=1)
        )
        turned = dot(la[2], jnp.concatenate([tall(minus_yz), tall(minus_zx)], axis=1))
        cell = u[rows, :]
        along = dot(wide(cell), rg[...])
        gain_yz = dot(la[5], tall(along[:, :LANES]))
        swap_yz = dot(la[6], tall(along[:, LANES:]))
        gain_zx = dot(la[3], tall(gains[2, rows, :]))
        swap_zx = dot(la[4], tall(gains[3, rows, :]))
        total = (gain_yz - cell) * straight[:, :LANES]
        total += swap_yz * turned[:, :LANES]
        total += (gains[0, rows, :] - cell) * straight[:, LANES : 2 * LANES]
        total += gains[1, rows, :] * straight[:, 3 * LANES :]
        total += (gain_zx - cell) * straight[:, 2 * LANES : 3 * LANES]
        total += swap_zx * turned[:, LANES:]
        v[rows, :] = total
        return carry

    lax.fori_loop(0, NV, third, 0, unroll=2)
    for x in range(NV):
        for c in range(cells):
            out[c, :, x * NV : (x + 1) * NV] = v[x * NV : (x + 1) * NV, c * HALF : c * HALF + NV]


def collide(cells):
    tables = build_tables()
    vmem = pl.BlockSpec(memory_space=pltpu.VMEM)
    size = (NV * NV, LANES)
    return pl.pallas_call(
        collide_kernel,
        out_shape=jax.ShapeDtypeStruct(cells.shape, jnp.float32),
        in_specs=[vmem, pl.BlockSpec(memory_space=pl.ANY)] + [vmem] * 5,
        out_specs=vmem,
        scratch_shapes=[
            pltpu.VMEM(size, jnp.float32),
            pltpu.VMEM(size, jnp.float32),
            pltpu.VMEM(size, jnp.float32),
            pltpu.VMEM(size, jnp.float32),
            pltpu.VMEM((6, NV, NV, LANES), jnp.float32),
            pltpu.VMEM((6,) + size, jnp.float32),
            pltpu.VMEM((4,) + size, jnp.float32),
            pltpu.SemaphoreType.DMA,
        ],
        compiler_params=pltpu.CompilerParams(vmem_limit_bytes=48 * 1024 * 1024),
        cost_estimate=pl.CostEstimate(
            flops=10**9, bytes_accessed=10 * 2**20, transcendentals=0
        ),
    )(cells, *[jnp.asarray(t) for t in tables])


def padded_2(cells, sides, width):
    for axis, dim in sides:
        count = lax.axis_size(axis)
        ends = count - 1
        head = lax.slice_in_dim(cells, 0, width, axis=dim)
        tail = lax.slice_in_dim(cells, cells.shape[dim] - width, cells.shape[dim], axis=dim)
        cells = jnp.concatenate(
            [
                lax.ppermute(tail, axis, [(i, (i + 1) % count) for i in range(ends)]),
                cells,
                lax.ppermute(head, axis, [((i + 1) % count, i) for i in range(ends)]),
            ],
            axis=dim,
        )
    return cells


def body(distribution, collision_rate, face_flags):
    cell_count, planes_dev, width = distribution.shape
    points = NV
    regrouped = lax.all_to_all(distribution, "vel", split_axis=0, concat_axis=1, tiled=True)
    own = regrouped.shape[0]
    terms = [collide(regrouped[i : min(i + 2, own)]) for i in range(0, own, 2)]
    cell_terms = terms[0] if len(terms) == 1 else jnp.concatenate(terms, axis=0)
    collision_term = lax.all_to_all(cell_terms, "vel", split_axis=1, concat_axis=0, tiled=True)
    offset = lax.axis_index("space") * cell_count
    padded = padded_2(distribution, (("space", 0),), 1)
    mirror = distribution.reshape(cell_count, planes_dev, points, points)[:, :, ::-1, :].reshape(
        cell_count, planes_dev, width
    )
    wall_flags = jnp.concatenate([face_flags, jnp.ones((1,), jnp.int32)])
    nearby_walls = lax.dynamic_slice_in_dim(wall_flags, offset, cell_count + 1)
    lower_wall = (nearby_walls[:-1] == 1)[:, None, None]
    upper_wall = (nearby_walls[1:] == 1)[:, None, None]
    at_start = (offset + jnp.arange(cell_count, dtype=jnp.int32) == 0)[:, None, None]
    lower_side = jnp.where(lower_wall, mirror, jnp.where(at_start, distribution, padded[:-2]))
    upper_side = jnp.where(upper_wall, mirror, padded[2:])
    column = (jnp.arange(width, dtype=jnp.int32) // points).astype(jnp.float32)
    centre = (points - 1) / 2.0
    speed = COURANT * (column - centre) / centre
    upwind_flux = jnp.where(
        speed > 0, speed * (distribution - lower_side), speed * (upper_side - distribution)
    )
    return distribution - upwind_flux + collision_rate[:, None, None] * collision_term


def solution(mesh):
    return jax.shard_map(
        body,
        mesh=mesh,
        in_specs=(P("space", "vel", None), P("space"), P()),
        out_specs=P("space", "vel", None),
        check_vma=False,
    )
```

```python
import math

import jax
import jax.numpy as jnp
import ml_dtypes
import numpy as np
from jax import lax
from jax.experimental import pallas as pl
from jax.experimental.pallas import tpu as pltpu
from jax.sharding import PartitionSpec as P

NV = 48
LENGTH = 8.0
RADIUS = 6.0
COURANT = 0.9
GOLDEN = (1.0 + math.sqrt(5.0)) / 2.0
SCALE = math.sqrt(1.0 + GOLDEN * GOLDEN)
HALF = 64
LANES = 128
BATCH = 4
BF = jnp.bfloat16


def real_basis():
    j = np.arange(NV)
    q = np.zeros((NV, NV))
    for f in range(25):
        q[f] = np.cos(2 * np.pi * f * j / NV) * (1.0 if f in (0, 24) else math.sqrt(2.0))
    for f in range(1, 24):
        q[24 + f] = np.sin(2 * np.pi * f * j / NV) * math.sqrt(2.0)
    q /= math.sqrt(NV)
    odd = np.zeros((NV, NV))
    for f in range(1, 24):
        odd[:, f] = -q[24 + f]
        odd[:, 24 + f] = q[f]
    mag = np.concatenate([np.arange(24), [0], np.arange(1, 24)]) * (math.pi / LENGTH)
    return q, odd, mag


def circulants():
    j = np.arange(NV)
    k = np.where(j < 24, j, np.where(j == 24, 0, j - NV))
    xi = k * (math.pi / LENGTH)
    f = np.fft.fft(np.eye(NV), axis=0)

    def real(mult):
        return np.real(np.fft.ifft(mult[:, None] * f, axis=0))

    result = []
    for length in (1.0 / SCALE, GOLDEN / SCALE):
        angle = 0.5 * RADIUS * xi * length
        result.append((real(np.cos(angle)), real(1j * np.sin(angle))))
    return result


def split_np(w):
    w = np.asarray(w, np.float32)
    hi = w.astype(ml_dtypes.bfloat16)
    lo = (w - hi.astype(np.float32)).astype(ml_dtypes.bfloat16)
    return hi, lo


def left(w):
    hi, lo = split_np(w)
    return np.concatenate([hi, hi, lo], axis=1)


def right(w):
    full = np.zeros((LANES, LANES))
    full[:NV, :NV] = w.T
    full[HALF : HALF + NV, HALF : HALF + NV] = w.T
    hi, lo = split_np(full)
    return np.concatenate([hi, hi, lo], axis=0)


def build_tables():
    q, odd, mag = real_basis()
    (c1, d1), (c2, d2) = circulants()
    mz, mx, my = mag[:, None, None], mag[None, :, None], mag[None, None, :]
    square = mz * mz + mx * mx + my * my

    def sinc(p):
        return np.sinc(RADIUS * np.sqrt(np.maximum(square - p * p, 0.0)) / (2.0 * math.pi))

    plus, minus = [], []
    for first, second in ((my, mz), (mx, my), (mz, mx)):
        same = sinc((first + GOLDEN * second) / SCALE)
        other = sinc((GOLDEN * second - first) / SCALE)
        plus.append((same + other) / 6.0)
        minus.append((other - same) / 6.0)
    spec = np.zeros((6, NV, NV, LANES), np.float32)
    values = np.stack(plus + minus)
    spec[..., :NV] = values
    spec[..., HALF : HALF + NV] = values
    lefts = [q, q.T, odd, c1, d1, c2, d2]
    left_all = np.stack([left(w) for w in lefts])
    left_pair = left(np.concatenate([c2, d2], axis=0))
    right_first = np.concatenate([right(w) for w in (q, c2, d2)], axis=1)
    right_rest = np.stack([right(q.T), right(odd)])
    right_gain = np.concatenate([right(c1), right(d1)], axis=1)
    return spec, left_all, left_pair, right_first, right_rest, right_gain


def parts(x):
    hi = x.astype(BF)
    lo = (x - hi.astype(jnp.float32)).astype(BF)
    return hi, lo


def tall(x):
    hi, lo = parts(x)
    return jnp.concatenate([hi, lo, hi], axis=0)


def wide(x):
    hi, lo = parts(x)
    return jnp.concatenate([hi, lo, hi], axis=1)


def dot(a, b):
    return jnp.dot(a, b, preferred_element_type=jnp.float32)


def each(w, x):
    blocks = [tall(x[i * NV : (i + 1) * NV]) for i in range(BATCH)]
    result = dot(w, jnp.concatenate(blocks, axis=1))
    return jnp.concatenate([result[:, i * LANES : (i + 1) * LANES] for i in range(BATCH)], axis=0)


def collide_kernel(
    u_in, spec_hbm, la, lp, rf, rr, rg, out, u, v, ey, fy, spec, fields, gains, sem
):
    cells = u_in.shape[0]
    load = pltpu.make_async_copy(spec_hbm, spec, sem)
    load.start()
    u[...] = jnp.zeros_like(u)
    for x in range(NV):
        for c in range(cells):
            u[x * NV : (x + 1) * NV, c * HALF : c * HALF + NV] = u_in[c, :, x * NV : (x + 1) * NV]

    def first(group, carry):
        start = pl.multiple_of(group * BATCH * NV, BATCH * NV)
        rows = pl.ds(start, BATCH * NV)
        three = dot(wide(u[rows, :]), rf[...])
        ey[rows, :] = three[:, LANES : 2 * LANES]
        fy[rows, :] = three[:, 2 * LANES :]
        v[rows, :] = each(la[0], three[:, :LANES])
        return carry

    lax.fori_loop(0, NV // BATCH, first, 0)
    load.wait()

    def second(z, carry):
        rows = pl.ds(z, NV, stride=NV)
        s = dot(la[0], tall(v[rows, :]))
        hat = [tall(s * spec[f, z]) for f in range(6)]
        even = dot(la[1], jnp.concatenate(hat[:4], axis=1))
        odd = dot(la[2], jnp.concatenate(hat[4:], axis=1))
        for f in range(4):
            fields[f, rows, :] = even[:, f * LANES : (f + 1) * LANES]
        for f in range(2):
            fields[4 + f, rows, :] = odd[:, f * LANES : (f + 1) * LANES]
        pair = dot(lp[...], tall(u[rows, :]))
        gains[0, rows, :] = dot(la[3], tall(ey[rows, :]))
        gains[1, rows, :] = dot(la[4], tall(fy[rows, :]))
        gains[2, rows, :] = pair[:NV]
        gains[3, rows, :] = pair[NV:]
        return carry

    lax.fori_loop(0, NV, second, 0, unroll=4)

    def third(group, carry):
        count = BATCH * NV
        start = pl.multiple_of(group * count, count)
        rows = pl.ds(start, count)
        even_in = [wide(fields[f, rows, :]) for f in (0, 1, 2, 5)]
        odd_in = [wide(fields[f, rows, :]) for f in (3, 4)]
        even = dot(jnp.concatenate(even_in, axis=0), rr[0])
        odd = dot(jnp.concatenate(odd_in, axis=0), rr[1])
        cell = u[rows, :]
        along = dot(wide(cell), rg[...])
        total = (each(la[5], along[:, :LANES]) - cell) * each(la[1], even[:count])
        total += each(la[6], along[:, LANES:]) * each(la[2], odd[:count])
        total += (gains[0, rows, :] - cell) * each(la[1], even[count : 2 * count])
        total += gains[1, rows, :] * each(la[1], odd[count:])
        total += (each(la[3], gains[2, rows, :]) - cell) * each(la[1], even[2 * count : 3 * count])
        total += each(la[4], gains[3, rows, :]) * each(la[2], even[3 * count :])
        v[rows, :] = total
        return carry

    lax.fori_loop(0, NV // BATCH, third, 0)
    for x in range(NV):
        for c in range(cells):
            out[c, :, x * NV : (x + 1) * NV] = v[x * NV : (x + 1) * NV, c * HALF : c * HALF + NV]


def collide(cells):
    tables = build_tables()
    vmem = pl.BlockSpec(memory_space=pltpu.VMEM)
    size = (NV * NV, LANES)
    return pl.pallas_call(
        collide_kernel,
        out_shape=jax.ShapeDtypeStruct(cells.shape, jnp.float32),
        in_specs=[vmem, pl.BlockSpec(memory_space=pl.ANY)] + [vmem] * 5,
        out_specs=vmem,
        scratch_shapes=[
            pltpu.VMEM(size, jnp.float32),
            pltpu.VMEM(size, jnp.float32),
            pltpu.VMEM(size, jnp.float32),
            pltpu.VMEM(size, jnp.float32),
            pltpu.VMEM((6, NV, NV, LANES), jnp.float32),
            pltpu.VMEM((6,) + size, jnp.float32),
            pltpu.VMEM((4,) + size, jnp.float32),
            pltpu.SemaphoreType.DMA,
        ],
        compiler_params=pltpu.CompilerParams(vmem_limit_bytes=48 * 1024 * 1024),
        cost_estimate=pl.CostEstimate(
            flops=10**9, bytes_accessed=10 * 2**20, transcendentals=0
        ),
    )(cells, *[jnp.asarray(t) for t in tables])


def padded_2(cells, sides, width):
    for axis, dim in sides:
        count = lax.axis_size(axis)
        ends = count - 1
        head = lax.slice_in_dim(cells, 0, width, axis=dim)
        tail = lax.slice_in_dim(cells, cells.shape[dim] - width, cells.shape[dim], axis=dim)
        cells = jnp.concatenate(
            [
                lax.ppermute(tail, axis, [(i, (i + 1) % count) for i in range(ends)]),
                cells,
                lax.ppermute(head, axis, [((i + 1) % count, i) for i in range(ends)]),
            ],
            axis=dim,
        )
    return cells


def body(distribution, collision_rate, face_flags):
    cell_count, planes_dev, width = distribution.shape
    points = NV
    regrouped = lax.all_to_all(distribution, "vel", split_axis=0, concat_axis=1, tiled=True)
    own = regrouped.shape[0]
    terms = [collide(regrouped[i : min(i + 2, own)]) for i in range(0, own, 2)]
    cell_terms = terms[0] if len(terms) == 1 else jnp.concatenate(terms, axis=0)
    collision_term = lax.all_to_all(cell_terms, "vel", split_axis=1, concat_axis=0, tiled=True)
    offset = lax.axis_index("space") * cell_count
    padded = padded_2(distribution, (("space", 0),), 1)
    mirror = distribution.reshape(cell_count, planes_dev, points, points)[:, :, ::-1, :].reshape(
        cell_count, planes_dev, width
    )
    wall_flags = jnp.concatenate([face_flags, jnp.ones((1,), jnp.int32)])
    nearby_walls = lax.dynamic_slice_in_dim(wall_flags, offset, cell_count + 1)
    lower_wall = (nearby_walls[:-1] == 1)[:, None, None]
    upper_wall = (nearby_walls[1:] == 1)[:, None, None]
    at_start = (offset + jnp.arange(cell_count, dtype=jnp.int32) == 0)[:, None, None]
    lower_side = jnp.where(lower_wall, mirror, jnp.where(at_start, distribution, padded[:-2]))
    upper_side = jnp.where(upper_wall, mirror, padded[2:])
    column = (jnp.arange(width, dtype=jnp.int32) // points).astype(jnp.float32)
    centre = (points - 1) / 2.0
    speed = COURANT * (column - centre) / centre
    upwind_flux = jnp.where(
        speed > 0, speed * (distribution - lower_side), speed * (upper_side - distribution)
    )
    return distribution - upwind_flux + collision_rate[:, None, None] * collision_term


def solution(mesh):
    return jax.shard_map(
        body,
        mesh=mesh,
        in_specs=(P("space", "vel", None), P("space"), P()),
        out_specs=P("space", "vel", None),
        check_vma=False,
    )
```

```python
import math

import jax
import jax.numpy as jnp
import ml_dtypes
import numpy as np
from jax import lax
from jax.experimental import pallas as pl
from jax.experimental.pallas import tpu as pltpu
from jax.sharding import PartitionSpec as P

NV = 48
LENGTH = 8.0
RADIUS = 6.0
COURANT = 0.9
GOLDEN = (1.0 + math.sqrt(5.0)) / 2.0
SCALE = math.sqrt(1.0 + GOLDEN * GOLDEN)
HALF = 64
LANES = 128
BATCH = 8
BF = jnp.bfloat16


def real_basis():
    j = np.arange(NV)
    q = np.zeros((NV, NV))
    for f in range(25):
        q[f] = np.cos(2 * np.pi * f * j / NV) * (1.0 if f in (0, 24) else math.sqrt(2.0))
    for f in range(1, 24):
        q[24 + f] = np.sin(2 * np.pi * f * j / NV) * math.sqrt(2.0)
    q /= math.sqrt(NV)
    odd = np.zeros((NV, NV))
    for f in range(1, 24):
        odd[:, f] = -q[24 + f]
        odd[:, 24 + f] = q[f]
    mag = np.concatenate([np.arange(24), [0], np.arange(1, 24)]) * (math.pi / LENGTH)
    return q, odd, mag


def circulants():
    j = np.arange(NV)
    k = np.where(j < 24, j, np.where(j == 24, 0, j - NV))
    xi = k * (math.pi / LENGTH)
    f = np.fft.fft(np.eye(NV), axis=0)

    def real(mult):
        return np.real(np.fft.ifft(mult[:, None] * f, axis=0))

    result = []
    for length in (1.0 / SCALE, GOLDEN / SCALE):
        angle = 0.5 * RADIUS * xi * length
        result.append((real(np.cos(angle)), real(1j * np.sin(angle))))
    return result


def split_np(w):
    w = np.asarray(w, np.float32)
    hi = w.astype(ml_dtypes.bfloat16)
    lo = (w - hi.astype(np.float32)).astype(ml_dtypes.bfloat16)
    return hi, lo


def left(w):
    hi, lo = split_np(w)
    return np.concatenate([hi, hi, lo], axis=1)


def right(w):
    full = np.zeros((LANES, LANES))
    full[:NV, :NV] = w.T
    full[HALF : HALF + NV, HALF : HALF + NV] = w.T
    hi, lo = split_np(full)
    return np.concatenate([hi, hi, lo], axis=0)


def build_tables():
    q, odd, mag = real_basis()
    (c1, d1), (c2, d2) = circulants()
    mz, mx, my = mag[:, None, None], mag[None, :, None], mag[None, None, :]
    square = mz * mz + mx * mx + my * my

    def sinc(p):
        return np.sinc(RADIUS * np.sqrt(np.maximum(square - p * p, 0.0)) / (2.0 * math.pi))

    plus, minus = [], []
    for first, second in ((my, mz), (mx, my), (mz, mx)):
        same = sinc((first + GOLDEN * second) / SCALE)
        other = sinc((GOLDEN * second - first) / SCALE)
        plus.append((same + other) / 6.0)
        minus.append((other - same) / 6.0)
    spec = np.zeros((6, NV, NV, LANES), np.float32)
    values = np.stack(plus + minus)
    spec[..., :NV] = values
    spec[..., HALF : HALF + NV] = values
    lefts = [q, q.T, odd, c1, d1, c2, d2]
    left_all = np.stack([left(w) for w in lefts])
    left_pair = left(np.concatenate([c2, d2], axis=0))
    right_first = np.concatenate([right(w) for w in (q, c2, d2)], axis=1)
    right_rest = np.stack([right(q.T), right(odd)])
    right_gain = np.concatenate([right(c1), right(d1)], axis=1)
    return spec, left_all, left_pair, right_first, right_rest, right_gain


def parts(x):
    hi = x.astype(BF)
    lo = (x - hi.astype(jnp.float32)).astype(BF)
    return hi, lo


def tall(x):
    hi, lo = parts(x)
    return jnp.concatenate([hi, lo, hi], axis=0)


def wide(x):
    hi, lo = parts(x)
    return jnp.concatenate([hi, lo, hi], axis=1)


def dot(a, b):
    return jnp.dot(a, b, preferred_element_type=jnp.float32)


def each(w, x):
    blocks = [tall(x[i * NV : (i + 1) * NV]) for i in range(BATCH)]
    result = dot(w, jnp.concatenate(blocks, axis=1))
    return jnp.concatenate([result[:, i * LANES : (i + 1) * LANES] for i in range(BATCH)], axis=0)


def collide_kernel(
    u_in, spec_hbm, la, lp, rf, rr, rg, out, u, v, ey, fy, spec, fields, gains, sem
):
    cells = u_in.shape[0]
    load = pltpu.make_async_copy(spec_hbm, spec, sem)
    load.start()
    u[...] = jnp.zeros_like(u)
    for x in range(NV):
        for c in range(cells):
            u[x * NV : (x + 1) * NV, c * HALF : c * HALF + NV] = u_in[c, :, x * NV : (x + 1) * NV]

    def first(group, carry):
        start = pl.multiple_of(group * BATCH * NV, BATCH * NV)
        rows = pl.ds(start, BATCH * NV)
        three = dot(wide(u[rows, :]), rf[...])
        ey[rows, :] = three[:, LANES : 2 * LANES]
        fy[rows, :] = three[:, 2 * LANES :]
        v[rows, :] = each(la[0], three[:, :LANES])
        return carry

    lax.fori_loop(0, NV // BATCH, first, 0)
    load.wait()

    def second(z, carry):
        rows = pl.ds(z, NV, stride=NV)
        s = dot(la[0], tall(v[rows, :]))
        hat = [tall(s * spec[f, z]) for f in range(6)]
        even = dot(la[1], jnp.concatenate(hat[:4], axis=1))
        odd = dot(la[2], jnp.concatenate(hat[4:], axis=1))
        for f in range(4):
            fields[f, rows, :] = even[:, f * LANES : (f + 1) * LANES]
        for f in range(2):
            fields[4 + f, rows, :] = odd[:, f * LANES : (f + 1) * LANES]
        pair = dot(lp[...], tall(u[rows, :]))
        gains[0, rows, :] = dot(la[3], tall(ey[rows, :]))
        gains[1, rows, :] = dot(la[4], tall(fy[rows, :]))
        gains[2, rows, :] = pair[:NV]
        gains[3, rows, :] = pair[NV:]
        return carry

    lax.fori_loop(0, NV, second, 0, unroll=4)

    def third(group, carry):
        count = BATCH * NV
        start = pl.multiple_of(group * count, count)
        rows = pl.ds(start, count)
        even_in = [wide(fields[f, rows, :]) for f in (0, 1, 2, 5)]
        odd_in = [wide(fields[f, rows, :]) for f in (3, 4)]
        even = dot(jnp.concatenate(even_in, axis=0), rr[0])
        odd = dot(jnp.concatenate(odd_in, axis=0), rr[1])
        cell = u[rows, :]
        along = dot(wide(cell), rg[...])
        total = (each(la[5], along[:, :LANES]) - cell) * each(la[1], even[:count])
        total += each(la[6], along[:, LANES:]) * each(la[2], odd[:count])
        total += (gains[0, rows, :] - cell) * each(la[1], even[count : 2 * count])
        total += gains[1, rows, :] * each(la[1], odd[count:])
        total += (each(la[3], gains[2, rows, :]) - cell) * each(la[1], even[2 * count : 3 * count])
        total += each(la[4], gains[3, rows, :]) * each(la[2], even[3 * count :])
        v[rows, :] = total
        return carry

    lax.fori_loop(0, NV // BATCH, third, 0)
    for x in range(NV):
        for c in range(cells):
            out[c, :, x * NV : (x + 1) * NV] = v[x * NV : (x + 1) * NV, c * HALF : c * HALF + NV]


def collide(cells):
    tables = build_tables()
    vmem = pl.BlockSpec(memory_space=pltpu.VMEM)
    size = (NV * NV, LANES)
    return pl.pallas_call(
        collide_kernel,
        out_shape=jax.ShapeDtypeStruct(cells.shape, jnp.float32),
        in_specs=[vmem, pl.BlockSpec(memory_space=pl.ANY)] + [vmem] * 5,
        out_specs=vmem,
        scratch_shapes=[
            pltpu.VMEM(size, jnp.float32),
            pltpu.VMEM(size, jnp.float32),
            pltpu.VMEM(size, jnp.float32),
            pltpu.VMEM(size, jnp.float32),
            pltpu.VMEM((6, NV, NV, LANES), jnp.float32),
            pltpu.VMEM((6,) + size, jnp.float32),
            pltpu.VMEM((4,) + size, jnp.float32),
            pltpu.SemaphoreType.DMA,
        ],
        compiler_params=pltpu.CompilerParams(vmem_limit_bytes=48 * 1024 * 1024),
        cost_estimate=pl.CostEstimate(
            flops=10**9, bytes_accessed=10 * 2**20, transcendentals=0
        ),
    )(cells, *[jnp.asarray(t) for t in tables])


def padded_2(cells, sides, width):
    for axis, dim in sides:
        count = lax.axis_size(axis)
        ends = count - 1
        head = lax.slice_in_dim(cells, 0, width, axis=dim)
        tail = lax.slice_in_dim(cells, cells.shape[dim] - width, cells.shape[dim], axis=dim)
        cells = jnp.concatenate(
            [
                lax.ppermute(tail, axis, [(i, (i + 1) % count) for i in range(ends)]),
                cells,
                lax.ppermute(head, axis, [((i + 1) % count, i) for i in range(ends)]),
            ],
            axis=dim,
        )
    return cells


def body(distribution, collision_rate, face_flags):
    cell_count, planes_dev, width = distribution.shape
    points = NV
    regrouped = lax.all_to_all(distribution, "vel", split_axis=0, concat_axis=1, tiled=True)
    own = regrouped.shape[0]
    terms = [collide(regrouped[i : min(i + 2, own)]) for i in range(0, own, 2)]
    cell_terms = terms[0] if len(terms) == 1 else jnp.concatenate(terms, axis=0)
    collision_term = lax.all_to_all(cell_terms, "vel", split_axis=1, concat_axis=0, tiled=True)
    offset = lax.axis_index("space") * cell_count
    padded = padded_2(distribution, (("space", 0),), 1)
    mirror = distribution.reshape(cell_count, planes_dev, points, points)[:, :, ::-1, :].reshape(
        cell_count, planes_dev, width
    )
    wall_flags = jnp.concatenate([face_flags, jnp.ones((1,), jnp.int32)])
    nearby_walls = lax.dynamic_slice_in_dim(wall_flags, offset, cell_count + 1)
    lower_wall = (nearby_walls[:-1] == 1)[:, None, None]
    upper_wall = (nearby_walls[1:] == 1)[:, None, None]
    at_start = (offset + jnp.arange(cell_count, dtype=jnp.int32) == 0)[:, None, None]
    lower_side = jnp.where(lower_wall, mirror, jnp.where(at_start, distribution, padded[:-2]))
    upper_side = jnp.where(upper_wall, mirror, padded[2:])
    column = (jnp.arange(width, dtype=jnp.int32) // points).astype(jnp.float32)
    centre = (points - 1) / 2.0
    speed = COURANT * (column - centre) / centre
    upwind_flux = jnp.where(
        speed > 0, speed * (distribution - lower_side), speed * (upper_side - distribution)
    )
    return distribution - upwind_flux + collision_rate[:, None, None] * collision_term


def solution(mesh):
    return jax.shard_map(
        body,
        mesh=mesh,
        in_specs=(P("space", "vel", None), P("space"), P()),
        out_specs=P("space", "vel", None),
        check_vma=False,
    )
```
